256 devices in a mesh: mom: 16 (over z, x_lo), en: 16 (over x_hi, y, core).
Axes of the slice: x: 4 (x_hi: 2, x_lo: 2; x = x_hi * 2 + x_lo), y: 4, z: 8, core: 2. Of those that a mesh axis runs over, the one named last changes fastest.
Arguments:
- greens: bfloat16 [32, 2, 2, 12, 12, 2048], P('mom', None, None, None, None, 'en'), may hold values from -6 to 6
- phonon_kernel: bfloat16 [32, 2, 2, 16], replicated, may hold values from -0.1875 to 0.1875
- coupling: bfloat16 [2, 2, 12, 12], replicated, may hold values from -1.75 to 1.75
- neighbours: int32 [2, 2], replicated, may hold values from 0 to 1
- transfer_table: int32 [32, 32], replicated, may hold values from 0 to 31, as said below
Outputs:
- self_energy: bfloat16 [32, 2, 2, 12, 12, 2048], P('mom', None, None, None, None, 'en')
The draws below stay inside these ranges and needn't reach their ends.
Inputs may be any that keep to these rules, and one draw needn't show every extreme that they name: `transfer_table`: every row and every column of the table holds each of 0 to 31 once.
All inputs are finite; a program needn't handle non-finite values.
Results may differ from the reference program's by a relative error of at most 0.0058.
Values may be sent and summed in bfloat16 or wider, within the bound.
A program may use at most 64 MiB of HBM per device.

```python
import jax
import jax.numpy as jnp
from jax import lax

ORB = 12
NBR = 2
LAGS = 16
ATOMS = 2
MOMENTUM_TOTAL = 32
ENERGIES = 2048


def draw_transfer_table(key, part):
    order = jax.random.permutation(jax.random.fold_in(key, 17), MOMENTUM_TOTAL).astype(jnp.int32)
    rows = jnp.arange(MOMENTUM_TOTAL, dtype=jnp.int32)
    offsets = (rows[:, None] - rows[None, :]) % MOMENTUM_TOTAL
    return order[offsets].astype(jnp.int32)


def with_ends(entries, key, low, high):
    shape = entries.shape
    index_at = [jax.random.randint(jax.random.fold_in(key, axis), (), 0, shape[axis]) for axis in range(len(shape))]
    entries = entries.at[tuple(index_at)].set(low)
    longest = shape.index(max(shape))
    index_at[longest] = (index_at[longest] + 1) % shape[longest]
    return entries.at[tuple(index_at)].set(high)


def shard_levels(stream_key, dims, shards, low, largest):
    factor_of = 1.0
    for dim, blocks in shards:
        draws = jax.random.uniform(jax.random.fold_in(jax.random.fold_in(stream_key, 6), dim), (blocks,), jnp.float32, low / len(shards), largest / len(shards))
        factor_of = factor_of * jnp.repeat(jnp.exp(draws), dims[dim] // blocks).reshape((-1,) + (1,) * (len(dims) - 1 - dim))
    return factor_of


def gaussian(stream_key, shape, spread, reach, split=(), kind=jnp.bfloat16):
    values = spread * jax.random.normal(stream_key, shape, jnp.float32)
    if split:
        values = values * shard_levels(stream_key, shape, split, -0.22, 0.18)
    return jnp.clip(values, -reach, reach).astype(kind)


def setup_inputs(seed: int = 0) -> dict:
    arg_keys = jax.random.split(jax.random.key(seed), 6)
    greens = gaussian(arg_keys[0], (MOMENTUM_TOTAL, ATOMS, 2, ORB, ORB, ENERGIES), 1.0, 6.0, ((0, 16), (5, 16)))
    phonon_kernel = gaussian(arg_keys[1], (MOMENTUM_TOTAL, ATOMS, NBR, LAGS), (LAGS * NBR * MOMENTUM_TOTAL) ** -0.5, 0.1875)
    coupling = gaussian(arg_keys[2], (ATOMS, NBR, ORB, ORB), ORB ** -0.5, 1.75)
    neighbours = with_ends(jax.random.randint(arg_keys[3], (ATOMS, NBR), 0, ATOMS), jax.random.fold_in(arg_keys[3], 1), 0, ATOMS - 1).astype(jnp.int32)
    transfer_table = draw_transfer_table(jax.random.fold_in(arg_keys[5], 71), 0)
    return dict(greens=greens, phonon_kernel=phonon_kernel, coupling=coupling, neighbours=neighbours, transfer_table=transfer_table)


def couple(green_block, neighbours, coupling):
    collected_blocks = jnp.take(green_block, neighbours, axis=0)
    half_width = jnp.einsum("anop,anrpse->anrose", coupling, collected_blocks, preferred_element_type=jnp.float32).astype(jnp.bfloat16)
    return jnp.einsum("qbiwjm,qbkj->qbiwkm", half_width, coupling, preferred_element_type=jnp.float32).astype(jnp.bfloat16)


def reference(greens, phonon_kernel, coupling, neighbours, transfer_table):
    length = ENERGIES + LAGS
    kernel_hat = jnp.fft.rfft(phonon_kernel.astype(jnp.float32), n=length, axis=-1)

    def advance(running, inputs):
        green_block, column = inputs
        weights = couple(green_block, neighbours, coupling).astype(jnp.float32)
        weights_hat = jnp.fft.rfft(weights, n=length, axis=-1)
        running = running + jnp.einsum("kanf,anrotf->karotf", kernel_hat[column], weights_hat)
        return running, None

    freqs = length // 2 + 1
    start_sum = jnp.zeros((MOMENTUM_TOTAL, ATOMS, 2, ORB, ORB, freqs), kernel_hat.dtype)
    summed, _ = lax.scan(advance, start_sum, (greens, transfer_table.T))
    result = jnp.fft.irfft(summed, n=length, axis=-1)[..., :ENERGIES]
    return result.astype(jnp.bfloat16)
```

```python
import functools

import jax
import jax.numpy as jnp
from jax import lax
from jax.experimental import pallas as pl
from jax.experimental.pallas import tpu as pltpu
from jax.sharding import PartitionSpec as P

MESH = pl.DeviceIdType.MESH
F32 = jnp.float32
BF16 = jnp.bfloat16
I32 = jnp.int32

ORB = 12
PAIRS = 144
HALF = 72
WIDE = 128
ORDER = (
    (4, 0), (3, 1), (5, 0), (2, 1), (4, 1), (6, 0), (3, 0), (5, 1),
    (2, 0), (6, 1), (1, 1), (7, 0), (1, 0), (7, 1), (0, 1),
)


def lane(shape):
    return lax.broadcasted_iota(I32, shape, len(shape) - 1)


def row(shape):
    return lax.broadcasted_iota(I32, shape, len(shape) - 2)


def pick(index, choices):
    out = choices[-1]
    for value in range(len(choices) - 2, -1, -1):
        out = jnp.where(index == value, choices[value], out)
    return out


def dot(a, b):
    return jnp.dot(a, b, preferred_element_type=F32)


def dot_t(a, b):
    return lax.dot_general(a, b, (((1,), (1,)), ((), ())), preferred_element_type=F32)


def kernel(
    nen, g_ref, ph_ref, c_ref, nb_ref, t_ref, out_ref,
    yt, send1, recv1, rim_out, rim_in, ga, tt, ohs, t0, kron, send2, recv2,
    send1_sem, recv1_sem, send2_sem, recv2_sem, rim_sems, local_sems,
):
    m = lax.axis_index("mom")
    q = lax.axis_index("en")
    z = m // 2
    x = m % 2
    up = lax.rem(q + 1, nen)
    down = lax.rem(q + nen - 1, nen)

    def peer(step):
        dz, dx = step
        return lax.rem(z + dz, 8) * 2 + lax.rem(x + dx, 2)

    barrier = pltpu.get_barrier_semaphore()
    for step in ORDER:
        pl.semaphore_signal(barrier, inc=1, device_id={"mom": peer(step)}, device_id_type=MESH)
    pl.semaphore_signal(barrier, inc=1, device_id={"en": up}, device_id_type=MESH)
    pl.semaphore_signal(barrier, inc=1, device_id={"en": down}, device_id_type=MESH)

    for r in range(2):
        for c in range(4):
            block = g_ref.at[c % 2, lax.rem(c // 2 + x, 2), r]
            for o in range(ORB):
                piece = block[o].astype(F32)
                if c:
                    piece = pltpu.roll(piece, 32 * c, 1)
                yt[r, c, o * ORB : (o + 1) * ORB, :] = piece

    place = lane((PAIRS, WIDE)) >> 4

    def packed(b, r):
        return pick(((place + (9 - b)) & 7) >> 1, [yt[r, c] for c in range(4)])

    odd = (place & 1) == 1
    first = [packed(0, r) for r in range(2)]
    rim_out[...] = jnp.where(odd, first[0], pltpu.roll(first[1], 16, 1)).astype(BF16)
    for r in range(2):
        send1[r] = first[r].astype(BF16)

    pl.semaphore_wait(barrier, 17)
    rim = pltpu.make_async_remote_copy(
        rim_out, rim_in, rim_sems.at[0], rim_sems.at[1], device_id={"en": up}, device_id_type=MESH
    )
    rim.start()

    for b in range(1, 8):
        for r in range(2):
            send1[2 * b + r] = packed(b, r).astype(BF16)

    rim.wait()
    below = jnp.where(q > 0, rim_in[...].astype(F32), 0.0)
    for r in range(2):
        part = below if r == 0 else pltpu.roll(below, WIDE - 16, 1)
        send1[r] = jnp.where(odd, part, send1[r].astype(F32)).astype(BF16)

    def leg(step, send, recv, send_sem, recv_sem):
        there = peer(step)
        return pltpu.make_async_remote_copy(
            send.at[there], recv.at[m], send_sem.at[there], recv_sem.at[m],
            device_id={"mom": there}, device_id_type=MESH,
        )

    def arrival(step, send, recv, send_sem, recv_sem):
        there = peer(step)
        return pltpu.make_async_remote_copy(
            send.at[there], recv.at[there], send_sem.at[there], recv_sem.at[there],
            device_id={"mom": there}, device_id_type=MESH,
        )

    leg1 = (send1, recv1, send1_sem, recv1_sem)
    leg2 = (send2, recv2, send2_sem, recv2_sem)
    for step in ORDER:
        leg(step, *leg1).start()
    own1 = pltpu.make_async_copy(send1.at[m], recv1.at[m], local_sems.at[0])
    own1.start()

    table = t_ref[...].astype(F32).astype(BF16)
    kk = row((32, WIDE))
    for v in range(2):
        for g in range(8):
            slot = lane((32, WIDE)) >> 5
            if v:
                slot = slot ^ 2
            spread = (kk == slot + 4 * g).astype(F32).astype(BF16)
            wanted = (lane((32, WIDE)) & 31).astype(F32)
            ohs[v, g * 32 : (g + 1) * 32, :] = (dot(table, spread) == wanted).astype(F32).astype(BF16)

    shifted = (lane((WIDE, WIDE)) - 16 * (z + 7)) & 127
    slot_match = (row((WIDE, WIDE)) >> 5) == (shifted >> 5)
    lag_at = ((lane((64, WIDE)) - 16 * (z + 7)) & 31)
    for an in range(4):
        select = jnp.where(row((64, WIDE)) == 16 * an + 16 - lag_at, 1.0, 0.0)
        select = jnp.where(lag_at == 0, 0.0, jnp.where(lag_at > 16, 0.0, select)).astype(BF16)
        lags = dot(ph_ref[...], select)
        lags = jnp.concatenate([lags] * 4, axis=0)
        lags = jnp.where(slot_match, lags, 0.0).astype(BF16)
        t0[an] = dot(ohs[nb_ref[an // 2, an % 2]], lags)

    def spread_rows(k, carry):
        at = pl.multiple_of((k // 8) * 128 + lax.rem(k + z, 8) * 16, 16)
        for an in range(4):
            for g in range(8):
                line = jnp.broadcast_to(t0[an, pl.ds(g * 32 + k, 1), :], (16, WIDE))
                line = pltpu.roll(line, 0, 1, stride=1, stride_axis=0)
                tt[an, pl.ds(at, 16), g * WIDE : (g + 1) * WIDE] = line.astype(BF16)
        return carry

    lax.fori_loop(0, 32, spread_rows, 0)

    high = row((PAIRS, ORB))
    small = lane((PAIRS, ORB))
    over = jnp.zeros((PAIRS, ORB), I32)
    for i in range(1, ORB):
        over += (high >= ORB * i).astype(I32)
    outer = (over == small).astype(F32).astype(BF16)
    inner = (high - ORB * over == small).astype(F32).astype(BF16)
    for an in range(4):
        block = c_ref[an // 2, an % 2]
        left = dot_t(dot(outer, block).astype(BF16), outer)
        right = dot_t(dot(inner, block).astype(BF16), inner)
        kron[an] = (left * right).astype(BF16)

    own1.wait()
    for step in ORDER:
        arrival(step, *leg1).wait_recv()

    lower = (((lane((PAIRS, WIDE)) - 16 * (z + 7)) & 127) < 64)
    for g in range(8):
        near = recv1[2 * g].astype(F32)
        far = recv1[2 * g + 1].astype(F32)
        ga[0, :, g * WIDE : (g + 1) * WIDE] = jnp.where(lower, near, far).astype(BF16)
        ga[1, :, g * WIDE : (g + 1) * WIDE] = jnp.where(lower, far, near).astype(BF16)

    done = []
    for a in range(2):
        total = None
        for n in range(2):
            an = 2 * a + n
            conv = dot_t(ga[nb_ref[a, n]], tt[an]).astype(BF16)
            term = dot(kron[an], conv)
            total = term if total is None else total + term
        done.append(total)

    place2 = lane((HALF, WIDE)) >> 4
    for g in range(4):
        tiles = []
        for c in range(4):
            tile = done[c % 2][HALF * (c // 2) : HALF * (c // 2 + 1), g * WIDE : (g + 1) * WIDE]
            tiles.append(pltpu.roll(tile, 32 * c, 1) if c else tile)
        for i in range(4):
            send2[4 * g + i] = pick(((place2 + 16 - z - 2 * i) & 7) >> 1, tiles).astype(BF16)

    for step in ORDER:
        leg(step, *leg2).start()
    own2 = pltpu.make_async_copy(send2.at[m], recv2.at[m], local_sems.at[1])
    own2.start()
    own2.wait()
    for step in ORDER:
        arrival(step, *leg2).wait_recv()

    mine = lax.rem(m, 4)
    for r in range(2):
        blocks = [recv2[2 * b + r].astype(F32) for b in range(8)]
        halves = []
        for c in range(8):
            merged = pick((place2 + 16 - c - 2 * mine) & 7, blocks)
            halves.append(pltpu.roll(merged, (16 * (16 - c - 2 * mine)) & 127, 1))
        for a in range(2):
            for k in range(2):
                whole = jnp.concatenate([halves[2 * a + k], halves[4 + 2 * a + k]], axis=0)
                out_ref[k, a, r] = whole.astype(BF16)

    for step in ORDER:
        leg(step, *leg1).wait_send()
        leg(step, *leg2).wait_send()


def local(greens, phonon_kernel, coupling, neighbours, transfer_table, *, nen):
    vmem = pl.BlockSpec(memory_space=pltpu.VMEM)
    out = pl.pallas_call(
        functools.partial(kernel, nen),
        out_shape=jax.ShapeDtypeStruct((2, 2, 2, PAIRS, WIDE), BF16),
        in_specs=[vmem, vmem, vmem, pl.BlockSpec(memory_space=pltpu.SMEM), vmem],
        out_specs=vmem,
        scratch_shapes=[
            pltpu.VMEM((2, 4, PAIRS, WIDE), F32),
            pltpu.VMEM((16, PAIRS, WIDE), BF16),
            pltpu.VMEM((16, PAIRS, WIDE), BF16),
            pltpu.VMEM((PAIRS, WIDE), BF16),
            pltpu.VMEM((PAIRS, WIDE), BF16),
            pltpu.VMEM((2, PAIRS, 8 * WIDE), BF16),
            pltpu.VMEM((4, 512, 8 * WIDE), BF16),
            pltpu.VMEM((2, 256, WIDE), BF16),
            pltpu.VMEM((4, 256, WIDE), F32),
            pltpu.VMEM((4, PAIRS, PAIRS), BF16),
            pltpu.VMEM((16, HALF, WIDE), BF16),
            pltpu.VMEM((16, HALF, WIDE), BF16),
            pltpu.SemaphoreType.DMA((16,)),
            pltpu.SemaphoreType.DMA((16,)),
            pltpu.SemaphoreType.DMA((16,)),
            pltpu.SemaphoreType.DMA((16,)),
            pltpu.SemaphoreType.DMA((2,)),
            pltpu.SemaphoreType.DMA((2,)),
        ],
        compiler_params=pltpu.CompilerParams(
            collective_id=0, has_side_effects=True, vmem_limit_bytes=32 * 2**20
        ),
    )(greens, phonon_kernel.reshape(32, 64), coupling, neighbours, transfer_table)
    return out.reshape(greens.shape)


def solution(mesh):
    spec = P("mom", None, None, None, None, "en")
    return jax.shard_map(
        functools.partial(local, nen=mesh.shape["en"]),
        mesh=mesh,
        in_specs=(spec, P(), P(), P(), P()),
        out_specs=spec,
        check_vma=False,
    )
```

```python
import functools

import jax
import jax.numpy as jnp
from jax import lax
from jax.experimental import pallas as pl
from jax.experimental.pallas import tpu as pltpu
from jax.sharding import PartitionSpec as P

MESH = pl.DeviceIdType.MESH
F32 = jnp.float32
BF16 = jnp.bfloat16
I32 = jnp.int32

ORB = 12
PAIRS = 144
HALF = 72
WIDE = 128
EARLY = 10
ORDER = (
    (4, 0), (3, 1), (5, 0), (2, 1), (4, 1), (6, 0), (3, 0), (5, 1),
    (2, 0), (6, 1), (1, 1), (7, 0), (1, 0), (7, 1), (0, 1),
)


def lane(shape):
    return lax.broadcasted_iota(I32, shape, len(shape) - 1)


def row(shape):
    return lax.broadcasted_iota(I32, shape, len(shape) - 2)


def pick(index, choices):
    out = choices[-1]
    for value in range(len(choices) - 2, -1, -1):
        out = jnp.where(index == value, choices[value], out)
    return out


def dot(a, b):
    return jnp.dot(a, b, preferred_element_type=F32)


def dot_t(a, b):
    return lax.dot_general(a, b, (((1,), (1,)), ((), ())), preferred_element_type=F32)


def kernel(
    nen, g_hbm, ph_hbm, c_hbm, nb_hbm, t_hbm, out_ref,
    g_ref, ph_ref, c_ref, nb_ref, t_ref,
    yt, send1, recv1, rim_out, rim_in, ga, tt, ohs, t0, kron, acc, send2, recv2,
    send1_sem, recv1_sem, send2_sem, recv2_sem, rim_sems, local_sems, load_sems,
):
    m = lax.axis_index("mom")
    q = lax.axis_index("en")
    z = m // 2
    x = m % 2
    up = lax.rem(q + 1, nen)
    down = lax.rem(q + nen - 1, nen)

    def peer(step):
        dz, dx = step
        return lax.rem(z + dz, 8) * 2 + lax.rem(x + dx, 2)

    barrier = pltpu.get_barrier_semaphore()
    for step in ORDER:
        pl.semaphore_signal(barrier, inc=1, device_id={"mom": peer(step)}, device_id_type=MESH)
    pl.semaphore_signal(barrier, inc=1, device_id={"en": up}, device_id_type=MESH)
    pl.semaphore_signal(barrier, inc=1, device_id={"en": down}, device_id_type=MESH)

    loads = [
        pltpu.make_async_copy(there, here, load_sems.at[i])
        for i, (there, here) in enumerate(
            [(g_hbm, g_ref), (ph_hbm, ph_ref), (c_hbm, c_ref), (nb_hbm, nb_ref), (t_hbm, t_ref)]
        )
    ]
    for load in loads:
        load.start()
    loads[0].wait()

    for c in range(4):
        both = g_ref[c % 2, lax.rem(c // 2 + x, 2)].astype(F32)
        for r in range(2):
            block = both[:, r, :]
            yt[r, c] = pltpu.roll(block, 32 * c, 1) if c else block

    place = lane((PAIRS, WIDE)) >> 4

    def packed(b, r):
        return pick(((place + (9 - b)) & 7) >> 1, [yt[r, c] for c in range(4)])

    odd = (place & 1) == 1
    first = [packed(0, r) for r in range(2)]
    rim_out[...] = jnp.where(odd, first[0], pltpu.roll(first[1], 16, 1)).astype(BF16)
    for r in range(2):
        send1[r] = first[r].astype(BF16)

    rim = pltpu.make_async_remote_copy(
        rim_out, rim_in, rim_sems.at[0], rim_sems.at[1], device_id={"en": up}, device_id_type=MESH
    )
    for b in range(1, 8):
        for r in range(2):
            send1[2 * b + r] = packed(b, r).astype(BF16)

    def leg(step, send, recv, send_sem, recv_sem):
        there = peer(step)
        return pltpu.make_async_remote_copy(
            send.at[there], recv.at[m], send_sem.at[there], recv_sem.at[m],
            device_id={"mom": there}, device_id_type=MESH,
        )

    def arrival(step, send, recv, send_sem, recv_sem):
        there = peer(step)
        return pltpu.make_async_remote_copy(
            send.at[there], recv.at[there], send_sem.at[there], recv_sem.at[there],
            device_id={"mom": there}, device_id_type=MESH,
        )

    leg1 = (send1, recv1, send1_sem, recv1_sem)
    leg2 = (send2, recv2, send2_sem, recv2_sem)
    for load in loads[1:]:
        load.wait()
    table = t_ref[...].astype(F32).astype(BF16)
    kk = row((32, WIDE))
    for v in range(2):
        for g in range(8):
            slot = lane((32, WIDE)) >> 5
            if v:
                slot = slot ^ 2
            spread = (kk == slot + 4 * g).astype(F32).astype(BF16)
            wanted = (lane((32, WIDE)) & 31).astype(F32)
            ohs[v, g * 32 : (g + 1) * 32, :] = (dot(table, spread) == wanted).astype(F32).astype(BF16)

    shifted = (lane((WIDE, WIDE)) - 16 * (z + 7)) & 127
    slot_match = (row((WIDE, WIDE)) >> 5) == (shifted >> 5)
    lag_at = ((lane((64, WIDE)) - 16 * (z + 7)) & 31)
    same = (row((32, 32)) == lane((32, 32))).astype(F32).astype(BF16)
    kernels = dot_t(same, ph_ref[...]).astype(BF16)
    for an in range(4):
        select = jnp.where(row((64, WIDE)) == 16 * an + 16 - lag_at, 1.0, 0.0)
        select = jnp.where(lag_at == 0, 0.0, jnp.where(lag_at > 16, 0.0, select)).astype(BF16)
        lags = dot(kernels, select)
        lags = jnp.concatenate([lags] * 4, axis=0)
        lags = jnp.where(slot_match, lags, 0.0).astype(BF16)
        t0[an] = dot(ohs[nb_ref[an // 2, an % 2]], lags)

    pl.semaphore_wait(barrier, 17)
    rim.start()
    own1 = pltpu.make_async_copy(send1.at[m], recv1.at[m], local_sems.at[0])

    def send_above(step):
        @pl.when(lax.rem(z + step[0], 8) != 0)
        def _():
            leg(step, *leg1).start()

    def send_lowest(step):
        @pl.when(lax.rem(z + step[0], 8) == 0)
        def _():
            leg(step, *leg1).start()

    for step in ORDER[:EARLY]:
        send_above(step)
    rim.wait()
    below = jnp.where(q > 0, rim_in[...].astype(F32), 0.0)
    for r in range(2):
        part = below if r == 0 else pltpu.roll(below, WIDE - 16, 1)
        send1[r] = jnp.where(odd, part, send1[r].astype(F32)).astype(BF16)
    for step in ORDER:
        send_lowest(step)
    own1.start()
    for step in ORDER[EARLY:]:
        send_above(step)

    def spread_rows(k, carry):
        at = pl.multiple_of((k // 8) * 128 + lax.rem(k + z, 8) * 16, 16)
        for an in range(4):
            for g in range(8):
                line = jnp.broadcast_to(t0[an, pl.ds(g * 32 + k, 1), :], (16, WIDE))
                line = pltpu.roll(line, 0, 1, stride=1, stride_axis=0)
                tt[an, g // 2, pl.ds(at, 16), (g % 2) * WIDE : (g % 2 + 1) * WIDE] = line.astype(BF16)
        return carry

    lax.fori_loop(0, 32, spread_rows, 0)

    high = row((PAIRS, ORB))
    small = lane((PAIRS, ORB))
    over = jnp.zeros((PAIRS, ORB), I32)
    for i in range(1, ORB):
        over += (high >= ORB * i).astype(I32)
    outer = (over == small).astype(F32).astype(BF16)
    inner = (high - ORB * over == small).astype(F32).astype(BF16)
    for an in range(4):
        block = c_ref[an // 2][:, an % 2, :]
        left = dot_t(dot(outer, block).astype(BF16), outer)
        right = dot_t(dot(inner, block).astype(BF16), inner)
        kron[an] = (left * right).astype(BF16)

    lower = ((lane((PAIRS, WIDE)) - 16 * (z + 7)) & 127) < 64
    for turn in (2, 1, 3, 0):
        part = lax.rem(z // 2 + turn, 4)
        for i in range(4):
            there = 4 * part + i

            def wait_there():
                pltpu.make_async_remote_copy(
                    send1.at[there], recv1.at[there], send1_sem.at[there], recv1_sem.at[there],
                    device_id={"mom": there}, device_id_type=MESH,
                ).wait_recv()

            if turn:
                wait_there()
            else:
                pl.when(there != m)(wait_there)
        if not turn:
            own1.wait()
        for g in range(2):
            near = recv1[4 * part + 2 * g].astype(F32)
            far = recv1[4 * part + 2 * g + 1].astype(F32)
            ga[0, :, g * WIDE : (g + 1) * WIDE] = jnp.where(lower, near, far).astype(BF16)
            ga[1, :, g * WIDE : (g + 1) * WIDE] = jnp.where(lower, far, near).astype(BF16)
        for an in range(4):
            term = dot_t(ga[nb_ref[an // 2, an % 2]], tt[an, part])
            acc[an] = term if turn == 2 else acc[an] + term

    done = []
    for a in range(2):
        done.append(
            dot(kron[2 * a], acc[2 * a].astype(BF16)) + dot(kron[2 * a + 1], acc[2 * a + 1].astype(BF16))
        )

    place2 = lane((HALF, WIDE)) >> 4
    for g in range(4):
        tiles = []
        for c in range(4):
            tile = done[c % 2][HALF * (c // 2) : HALF * (c // 2 + 1), g * WIDE : (g + 1) * WIDE]
            tiles.append(pltpu.roll(tile, 32 * c, 1) if c else tile)
        for i in range(4):
            send2[4 * g + i] = pick(((place2 + 16 - z - 2 * i) & 7) >> 1, tiles).astype(BF16)

    for step in ORDER:
        leg(step, *leg2).start()
    own2 = pltpu.make_async_copy(send2.at[m], recv2.at[m], local_sems.at[1])
    own2.start()
    own2.wait()
    for step in ORDER:
        arrival(step, *leg2).wait_recv()

    mine = lax.rem(m, 4)
    for r in range(2):
        blocks = [recv2[2 * b + r].astype(F32) for b in range(8)]
        halves = []
        for c in range(8):
            merged = pick((place2 + 16 - c - 2 * mine) & 7, blocks)
            halves.append(pltpu.roll(merged, (16 * (16 - c - 2 * mine)) & 127, 1))
        for a in range(2):
            for k in range(2):
                whole = jnp.concatenate([halves[2 * a + k], halves[4 + 2 * a + k]], axis=0)
                out_ref[k, a, r] = whole.astype(BF16)

    for step in ORDER:
        leg(step, *leg1).wait_send()
        leg(step, *leg2).wait_send()


def local(greens, phonon_kernel, coupling, neighbours, transfer_table, *, nen):
    vmem = pl.BlockSpec(memory_space=pltpu.VMEM)
    hbm = pl.BlockSpec(memory_space=pltpu.HBM)
    arguments = (
        greens.transpose(0, 1, 3, 4, 2, 5).reshape(2, 2, PAIRS, 2, WIDE),
        phonon_kernel.transpose(1, 2, 3, 0).reshape(64, 32),
        coupling.transpose(0, 2, 1, 3),
        neighbours,
        transfer_table,
    )
    out = pl.pallas_call(
        functools.partial(kernel, nen),
        out_shape=jax.ShapeDtypeStruct((2, 2, 2, PAIRS, WIDE), BF16),
        in_specs=[hbm] * 5,
        out_specs=vmem,
        scratch_shapes=[
            pltpu.VMEM((2, 2, PAIRS, 2, WIDE), BF16),
            pltpu.VMEM((64, 32), BF16),
            pltpu.VMEM((2, ORB, 2, ORB), BF16),
            pltpu.SMEM((2, 2), I32),
            pltpu.VMEM((32, 32), I32),
            pltpu.VMEM((2, 4, PAIRS, WIDE), F32),
            pltpu.VMEM((16, PAIRS, WIDE), BF16),
            pltpu.VMEM((16, PAIRS, WIDE), BF16),
            pltpu.VMEM((PAIRS, WIDE), BF16),
            pltpu.VMEM((PAIRS, WIDE), BF16),
            pltpu.VMEM((2, PAIRS, 2 * WIDE), BF16),
            pltpu.VMEM((4, 4, 512, 2 * WIDE), BF16),
            pltpu.VMEM((2, 256, WIDE), BF16),
            pltpu.VMEM((4, 256, WIDE), F32),
            pltpu.VMEM((4, PAIRS, PAIRS), BF16),
            pltpu.VMEM((4, PAIRS, 512), F32),
            pltpu.VMEM((16, HALF, WIDE), BF16),
            pltpu.VMEM((16, HALF, WIDE), BF16),
            pltpu.SemaphoreType.DMA((16,)),
            pltpu.SemaphoreType.DMA((16,)),
            pltpu.SemaphoreType.DMA((16,)),
            pltpu.SemaphoreType.DMA((16,)),
            pltpu.SemaphoreType.DMA((2,)),
            pltpu.SemaphoreType.DMA((2,)),
            pltpu.SemaphoreType.DMA((5,)),
        ],
        compiler_params=pltpu.CompilerParams(
            collective_id=0, has_side_effects=True, vmem_limit_bytes=67_043_328
        ),
    )(*arguments)
    return out.reshape(greens.shape)


def solution(mesh):
    spec = P("mom", None, None, None, None, "en")
    return jax.shard_map(
        functools.partial(local, nen=mesh.shape["en"]),
        mesh=mesh,
        in_specs=(spec, P(), P(), P(), P()),
        out_specs=spec,
        check_vma=False,
    )
```

```python
import functools

import jax
import jax.numpy as jnp
from jax import lax
from jax.experimental import pallas as pl
from jax.experimental.pallas import tpu as pltpu
from jax.sharding import PartitionSpec as P

MESH = pl.DeviceIdType.MESH
F32 = jnp.float32
BF16 = jnp.bfloat16
I32 = jnp.int32

ORB = 12
PAIRS = 144
HALF = 72
WIDE = 128
LOWEST = 6
OPEN = 0
AROUND = (4, 3, 5, 2, 6, 1, 7, 0)


def order(z):
    return 4 * (z % 2) + (z // 2 + 1) % 4


def lane(shape):
    return lax.broadcasted_iota(I32, shape, len(shape) - 1)


def row(shape):
    return lax.broadcasted_iota(I32, shape, len(shape) - 2)


def pick(index, choices):
    out = choices[-1]
    for value in range(len(choices) - 2, -1, -1):
        out = jnp.where(index == value, choices[value], out)
    return out


def dot(a, b):
    return jnp.dot(a, b, preferred_element_type=F32)


def dot_t(a, b):
    return lax.dot_general(a, b, (((1,), (1,)), ((), ())), preferred_element_type=F32)


def kernel(
    nen, g_hbm, ph_hbm, c_hbm, nb_hbm, t_hbm, out_ref,
    g_ref, ph_ref, c_ref, nb_ref, t_ref,
    yt, parcel, lows, highs, ga, tt, ohs, t0, kron, acc, send2, recv2,
    home_sem, below_sem, low_sem, high_sem, pass_sem, send2_sem, recv2_sem, load_sems, open_sem,
):
    m = lax.axis_index("mom")
    q = lax.axis_index("en")
    z = m // 2
    w = order(z)
    x = m % 2
    core = q % 2
    pair = q // 2
    pairs = nen // 2
    chunk = lax.rem(2 * w + core, 8)
    holder = w // 4

    def place_of(there, pair_there, core_there):
        return {"mom": there, "en": 2 * pair_there + core_there}

    barrier = pltpu.get_barrier_semaphore()

    def greet(there, pair_there, core_there):
        pl.semaphore_signal(
            barrier, inc=1, device_id=place_of(there, pair_there, core_there), device_id_type=MESH
        )

    after = lax.rem(pair + 1, pairs)
    before = lax.rem(pair + pairs - 1, pairs)
    for step in range(1, 16):
        for c in range(2):
            greet(lax.rem(m + step, 16), pair, c)
    greet(m, pair, 1 - core)

    beside = jnp.where(core == 0, before, after)
    greet(m, beside, 1 - core)

    loads = [
        pltpu.make_async_copy(there, here, load_sems.at[i])
        for i, (there, here) in enumerate(
            [(g_hbm, g_ref), (ph_hbm, ph_ref), (c_hbm, c_ref), (nb_hbm, nb_ref), (t_hbm, t_ref)]
        )
    ]
    for load in loads:
        load.start()
    loads[0].wait()

    for c in range(4):
        both = g_ref[c % 2, lax.rem(c // 2 + x, 2)].astype(F32)
        for r in range(2):
            block = both[:, r, :]
            yt[r, c] = pltpu.roll(block, 32 * c, 1) if c else block

    place = lane((HALF, WIDE)) >> 4
    for r in range(2):
        for g in range(8):
            at = ((place + (8 - g)) & 7) >> 1
            upper = pick(at, [yt[r, c, :HALF, :] for c in range(4)])
            lower = pick(at, [yt[r, c, HALF:, :] for c in range(4)])
            parcel[r, g] = jnp.where(((place + g) & 1) == 0, upper, pltpu.roll(lower, 16, 1)).astype(BF16)

    for load in loads[1:]:
        load.wait()
    table = t_ref[...].astype(F32).astype(BF16)
    kk = row((32, WIDE))
    for v in range(2):
        for g in range(8):
            slot = lane((32, WIDE)) >> 5
            if v:
                slot = slot ^ 2
            spread = (kk == slot + 4 * g).astype(F32).astype(BF16)
            wanted = (lane((32, WIDE)) & 31).astype(F32)
            ohs[v, g * 32 : (g + 1) * 32, :] = (dot(table, spread) == wanted).astype(F32).astype(BF16)

    shifted = (lane((WIDE, WIDE)) - 16 * (chunk + 7)) & 127
    slot_match = (row((WIDE, WIDE)) >> 5) == (shifted >> 5)
    lag_at = ((lane((64, WIDE)) - 16 * (chunk + 7)) & 31)
    same = (row((32, 32)) == lane((32, 32))).astype(F32).astype(BF16)
    kernels = dot_t(same, ph_ref[...]).astype(BF16)
    for an in range(4):
        select = jnp.where(row((64, WIDE)) == 16 * an + 16 - lag_at, 1.0, 0.0)
        select = jnp.where(lag_at == 0, 0.0, jnp.where(lag_at > 16, 0.0, select)).astype(BF16)
        lags = dot(kernels, select)
        lags = jnp.concatenate([lags] * 4, axis=0)
        lags = jnp.where(slot_match, lags, 0.0).astype(BF16)
        t0[an] = dot(ohs[nb_ref[an // 2, an % 2]], lags)

    pl.semaphore_wait(barrier, 32)

    @pl.when(jnp.logical_and(core == 0, pair != 0))
    def _():
        pl.semaphore_signal(open_sem, inc=1, device_id=place_of(m, before, 1), device_id_type=MESH)

    def remote(source, target, send_sem, recv_sem, there):
        return pltpu.make_async_remote_copy(
            source, target, send_sem, recv_sem, device_id=there, device_id_type=MESH
        )

    def send_high(there, r, c):
        g = lax.rem(2 * order(there) + c, 8)
        return remote(
            parcel.at[r, g], highs.at[m], home_sem.at[r, g], high_sem.at[m], place_of(2 * there + r, pair, c)
        )

    def send_low(there, r):
        g = (2 * order(there) + 7) % 8
        return remote(
            parcel.at[r, g], lows.at[m], below_sem.at[r, g], low_sem.at[m],
            place_of(2 * there + r, after if isinstance(there, int) else pair, 0),
        )

    def first_leg(act, own):
        for turn, dz in enumerate(AROUND):
            there = lax.rem(z + dz, 8)
            holds_high = order(there) // 4 == core
            holds_low = jnp.logical_and(lax.rem(order(there) + 7, 8) // 4 == core, order(there) != 0)
            for dx in (1, 0):
                r = lax.rem(x + dx, 2)
                same = dz == 0 and dx == 0

                @pl.when(holds_high)
                def _():
                    for c in range(2):
                        if same:
                            pl.when(core != c)(lambda c=c: act(send_high(there, r, c)))
                        else:
                            act(send_high(there, r, c))

                @pl.when(jnp.logical_and(holds_low, core == 1) if same else holds_low)
                def _():
                    act(send_low(there, r))

            if turn == OPEN:

                @pl.when(jnp.logical_and(core == 1, pair != pairs - 1))
                def _():
                    if own:
                        pl.semaphore_wait(open_sem, 1)
                    for r in range(2):
                        act(send_low(LOWEST, r))

        if own:

            @pl.when(holder == core)
            def _():
                pltpu.make_async_copy(parcel.at[x, chunk], highs.at[m], high_sem.at[m]).start()

            @pl.when(jnp.logical_and(core == 0, jnp.logical_and(w > 0, w < 5)))
            def _():
                pltpu.make_async_copy(parcel.at[x, lax.rem(2 * w + 7, 8)], lows.at[m], low_sem.at[m]).start()

    first_leg(lambda copy: copy.start(), True)

    def spread_rows(k, carry):
        at = pl.multiple_of((k // 8) * 128 + lax.rem(k + chunk, 8) * 16, 16)
        for an in range(4):
            for g in range(8):
                line = jnp.broadcast_to(t0[an, pl.ds(g * 32 + k, 1), :], (16, WIDE))
                line = pltpu.roll(line, 0, 1, stride=1, stride_axis=0)
                tt[an, g // 2, pl.ds(at, 16), (g % 2) * WIDE : (g % 2 + 1) * WIDE] = line.astype(BF16)
        return carry

    lax.fori_loop(0, 32, spread_rows, 0)

    high = row((PAIRS, ORB))
    small = lane((PAIRS, ORB))
    over = jnp.zeros((PAIRS, ORB), I32)
    for i in range(1, ORB):
        over += (high >= ORB * i).astype(I32)
    outer = (over == small).astype(F32).astype(BF16)
    inner = (high - ORB * over == small).astype(F32).astype(BF16)
    for an in range(4):
        block = c_ref[an // 2][:, an % 2, :]
        left = dot_t(dot(outer, block).astype(BF16), outer)
        right = dot_t(dot(inner, block).astype(BF16), inner)
        kron[an] = (left * right).astype(BF16)

    start = jnp.logical_and(jnp.logical_and(w == 0, core == 0), pair == 0)

    def passed_on(there):
        return remote(
            highs.at[there], lows.at[there], pass_sem.at[there], low_sem.at[there], place_of(m, pair, 1)
        )

    def arrived(buffer, sem, there):
        pltpu.make_async_copy(buffer.at[there], buffer.at[there], sem.at[there]).wait()

    even = ((place + chunk) & 1) == 1
    first_half = ((lane((PAIRS, WIDE)) - 16 * (chunk + 7)) & 127) < 64

    def merged(there):
        under = jnp.where(start, 0.0, lows[there].astype(F32))
        over = highs[there].astype(F32)
        upper = jnp.where(even, under, over)
        lower = pltpu.roll(jnp.where(even, over, under), WIDE - 16, 1)
        return jnp.concatenate([upper, lower], axis=0)

    def take(part):
        for i in range(4):
            arrived(highs, high_sem, 4 * part + i)

        @pl.when(core == 0)
        def _():
            for i in range(4):
                passed_on(4 * part + i).start()

    def convolve(part, fresh):
        for i in range(4):
            pl.when(jnp.logical_not(start))(lambda i=i: arrived(lows, low_sem, 4 * part + i))
        for g in range(2):
            near = merged(4 * part + 2 * g)
            far = merged(4 * part + 2 * g + 1)
            ga[0, :, g * WIDE : (g + 1) * WIDE] = jnp.where(first_half, near, far).astype(BF16)
            ga[1, :, g * WIDE : (g + 1) * WIDE] = jnp.where(first_half, far, near).astype(BF16)
        for an in range(4):
            term = dot_t(ga[nb_ref[an // 2, an % 2]], tt[an, part])
            acc[an] = term if fresh else acc[an] + term

    parts = [lax.rem(z // 2 + turn, 4) for turn in (2, 1, 3, 0)]
    take(parts[0])
    for i in range(4):
        if i < 3:
            take(parts[i + 1])
        convolve(parts[i], i == 0)

    slot = 2 * chunk + x

    def back(there):
        return remote(
            send2.at[there], recv2.at[slot], send2_sem.at[there], recv2_sem.at[slot],
            place_of(there, pair, holder),
        )

    for g in (0, 1, 2, 3):
        done = []
        for a in range(2):
            total = None
            for an in (2 * a, 2 * a + 1):
                term = dot(kron[an], acc[an, :, g * WIDE : (g + 1) * WIDE].astype(BF16))
                total = term if total is None else total + term
            done.append(total)
        tiles = []
        for c in range(4):
            block = done[c % 2][HALF * (c // 2) : HALF * (c // 2 + 1)]
            tiles.append(pltpu.roll(block, 32 * c, 1) if c else block)
        for i in (0, 1, 2, 3):
            send2[4 * g + i] = pick(((place + 16 - chunk - 2 * i) & 7) >> 1, tiles).astype(BF16)
        for there in [4 * g + i for i in (0, 1, 2, 3)]:
            here = jnp.logical_and(m == there, holder == core)

            @pl.when(jnp.logical_not(here))
            def _():
                back(there).start()

            @pl.when(here)
            def _():
                pltpu.make_async_copy(send2.at[there], recv2.at[slot], recv2_sem.at[slot]).start()

    for there in range(16):
        arrived(recv2, recv2_sem, there)

    mine = lax.rem(m, 4)
    for r in range(2):
        blocks = [recv2[2 * b + r].astype(F32) for b in range(8)]
        halves = []
        for c in range(8):
            merged = pick((place + 16 - c - 2 * mine) & 7, blocks)
            halves.append(pltpu.roll(merged, (16 * (16 - c - 2 * mine)) & 127, 1))
        for a in range(2):
            for k in range(2):
                whole = jnp.concatenate([halves[2 * a + k], halves[4 + 2 * a + k]], axis=0)
                out_ref[k, a, r] = whole.astype(BF16)

    first_leg(lambda copy: copy.wait_send(), False)
    for there in range(16):

        @pl.when(jnp.logical_not(jnp.logical_and(m == there, holder == core)))
        def _():
            back(there).wait_send()


    @pl.when(core == 0)
    def _():
        for there in range(16):
            passed_on(there).wait_send()


def local(greens, phonon_kernel, coupling, neighbours, transfer_table, *, nen):
    vmem = pl.BlockSpec(memory_space=pltpu.VMEM)
    hbm = pl.BlockSpec(memory_space=pltpu.HBM)
    arguments = (
        greens.transpose(0, 1, 3, 4, 2, 5).reshape(2, 2, PAIRS, 2, WIDE),
        phonon_kernel.transpose(1, 2, 3, 0).reshape(64, 32),
        coupling.transpose(0, 2, 1, 3),
        neighbours,
        transfer_table,
    )
    out = pl.pallas_call(
        functools.partial(kernel, nen),
        out_shape=jax.ShapeDtypeStruct((2, 2, 2, PAIRS, WIDE), BF16),
        in_specs=[hbm] * 5,
        out_specs=vmem,
        scratch_shapes=[
            pltpu.VMEM((2, 2, PAIRS, 2, WIDE), BF16),
            pltpu.VMEM((64, 32), BF16),
            pltpu.VMEM((2, ORB, 2, ORB), BF16),
            pltpu.SMEM((2, 2), I32),
            pltpu.VMEM((32, 32), I32),
            pltpu.VMEM((2, 4, PAIRS, WIDE), F32),
            pltpu.VMEM((2, 8, HALF, WIDE), BF16),
            pltpu.VMEM((16, HALF, WIDE), BF16),
            pltpu.VMEM((16, HALF, WIDE), BF16),
            pltpu.VMEM((2, PAIRS, 2 * WIDE), BF16),
            pltpu.VMEM((4, 4, 512, 2 * WIDE), BF16),
            pltpu.VMEM((2, 256, WIDE), BF16),
            pltpu.VMEM((4, 256, WIDE), F32),
            pltpu.VMEM((4, PAIRS, PAIRS), BF16),
            pltpu.VMEM((4, PAIRS, 512), F32),
            pltpu.VMEM((16, HALF, WIDE), BF16),
            pltpu.VMEM((16, HALF, WIDE), BF16),
            pltpu.SemaphoreType.DMA((2, 8)),
            pltpu.SemaphoreType.DMA((2, 8)),
            pltpu.SemaphoreType.DMA((16,)),
            pltpu.SemaphoreType.DMA((16,)),
            pltpu.SemaphoreType.DMA((16,)),
            pltpu.SemaphoreType.DMA((16,)),
            pltpu.SemaphoreType.DMA((16,)),
            pltpu.SemaphoreType.DMA((5,)),
            pltpu.SemaphoreType.REGULAR,
        ],
        compiler_params=pltpu.CompilerParams(
            collective_id=0, has_side_effects=True, vmem_limit_bytes=32 * 2**20
        ),
    )(*(pltpu.with_memory_space_constraint(value, pltpu.HBM) for value in arguments))
    return out.reshape(greens.shape)


def solution(mesh):
    spec = P("mom", None, None, None, None, "en")
    return jax.shard_map(
        functools.partial(local, nen=mesh.shape["en"]),
        mesh=mesh,
        in_specs=(spec, P(), P(), P(), P()),
        out_specs=spec,
        check_vma=False,
    )
```

```python
import functools

import jax
import jax.numpy as jnp
from jax import lax
from jax.experimental import pallas as pl
from jax.experimental.pallas import tpu as pltpu
from jax.sharding import PartitionSpec as P

MESH = pl.DeviceIdType.MESH
F32 = jnp.float32
BF16 = jnp.bfloat16
I32 = jnp.int32

ORB = 12
PAIRS = 144
HALF = 72
WIDE = 128
LOWEST = 6
OPEN = 1
AROUND = (4, 3, 5, 2, 6, 1, 7, 0)


def order(z):
    return 4 * (z % 2) + (z // 2 + 1) % 4


def lane(shape):
    return lax.broadcasted_iota(I32, shape, len(shape) - 1)


def row(shape):
    return lax.broadcasted_iota(I32, shape, len(shape) - 2)


def pick(index, choices):
    out = choices[-1]
    for value in range(len(choices) - 2, -1, -1):
        out = jnp.where(index == value, choices[value], out)
    return out


def dot(a, b):
    return jnp.dot(a, b, preferred_element_type=F32)


def dot_t(a, b):
    return lax.dot_general(a, b, (((1,), (1,)), ((), ())), preferred_element_type=F32)


def kernel(
    nen, g_hbm, ph_hbm, c_hbm, nb_hbm, t_hbm, out_ref,
    g_ref, ph_ref, c_ref, nb_ref, t_ref,
    yt, parcel, lows, highs, ga, tt, ohs, t0, kron, acc, send2, recv2,
    home_sem, below_sem, low_sem, high_sem, pass_sem, send2_sem, recv2_sem, load_sems, open_sem,
):
    m = lax.axis_index("mom")
    q = lax.axis_index("en")
    z = m // 2
    w = order(z)
    x = m % 2
    core = q % 2
    pair = q // 2
    pairs = nen // 2
    chunk = lax.rem(2 * w + core, 8)
    holder = w // 4

    def place_of(there, pair_there, core_there):
        return {"mom": there, "en": 2 * pair_there + core_there}

    barrier = pltpu.get_barrier_semaphore()

    def greet(there, pair_there, core_there):
        pl.semaphore_signal(
            barrier, inc=1, device_id=place_of(there, pair_there, core_there), device_id_type=MESH
        )

    after = lax.rem(pair + 1, pairs)
    before = lax.rem(pair + pairs - 1, pairs)
    for dz in AROUND[:-1]:
        for dx in range(2):
            for c in range(2):
                greet(lax.rem(z + dz, 8) * 2 + lax.rem(x + dx, 2), pair, c)
    for c in range(2):
        greet(2 * z + 1 - x, pair, c)
    greet(m, pair, 1 - core)

    beside = jnp.where(core == 0, before, after)
    linked = jnp.where(core == 0, pair != 0, pair != pairs - 1)

    @pl.when(linked)
    def _():
        greet(m, beside, 1 - core)


    loads = [
        pltpu.make_async_copy(there, here, load_sems.at[i])
        for i, (there, here) in enumerate(
            [(g_hbm, g_ref), (ph_hbm, ph_ref), (c_hbm, c_ref), (nb_hbm, nb_ref), (t_hbm, t_ref)]
        )
    ]
    for load in loads:
        load.start()
    loads[0].wait()

    for c in range(4):
        both = g_ref[c % 2, lax.rem(c // 2 + x, 2)].astype(F32)
        for r in range(2):
            block = both[:, r, :]
            yt[r, c] = pltpu.roll(block, 32 * c, 1) if c else block

    place = lane((HALF, WIDE)) >> 4
    for r in range(2):
        for g in range(8):
            at = ((place + (8 - g)) & 7) >> 1
            upper = pick(at, [yt[r, c, :HALF, :] for c in range(4)])
            lower = pick(at, [yt[r, c, HALF:, :] for c in range(4)])
            parcel[r, g] = jnp.where(((place + g) & 1) == 0, upper, pltpu.roll(lower, 16, 1)).astype(BF16)

    for load in loads[1:]:
        load.wait()
    table = t_ref[...].astype(F32).astype(BF16)
    kk = row((32, WIDE))
    for v in range(2):
        for g in range(8):
            slot = lane((32, WIDE)) >> 5
            if v:
                slot = slot ^ 2
            spread = (kk == slot + 4 * g).astype(F32).astype(BF16)
            wanted = (lane((32, WIDE)) & 31).astype(F32)
            ohs[v, g * 32 : (g + 1) * 32, :] = (dot(table, spread) == wanted).astype(F32).astype(BF16)

    shifted = (lane((WIDE, WIDE)) - 16 * (chunk + 7)) & 127
    slot_match = (row((WIDE, WIDE)) >> 5) == (shifted >> 5)
    lag_at = ((lane((64, WIDE)) - 16 * (chunk + 7)) & 31)
    same = (row((32, 32)) == lane((32, 32))).astype(F32).astype(BF16)
    kernels = dot_t(same, ph_ref[...]).astype(BF16)
    for an in range(4):
        select = jnp.where(row((64, WIDE)) == 16 * an + 16 - lag_at, 1.0, 0.0)
        select = jnp.where(lag_at == 0, 0.0, jnp.where(lag_at > 16, 0.0, select)).astype(BF16)
        lags = dot(kernels, select)
        lags = jnp.concatenate([lags] * 4, axis=0)
        lags = jnp.where(slot_match, lags, 0.0).astype(BF16)
        t0[an] = dot(ohs[nb_ref[an // 2, an % 2]], lags)

    pl.semaphore_wait(barrier, 31 + linked.astype(I32))


    @pl.when(jnp.logical_and(core == 0, pair != 0))
    def _():
        pl.semaphore_signal(open_sem, inc=1, device_id=place_of(m, before, 1), device_id_type=MESH)

    def remote(source, target, send_sem, recv_sem, there):
        return pltpu.make_async_remote_copy(
            source, target, send_sem, recv_sem, device_id=there, device_id_type=MESH
        )

    def send_high(there, r, c):
        g = lax.rem(2 * order(there) + c, 8)
        return remote(
            parcel.at[r, g], highs.at[m], home_sem.at[r, g], high_sem.at[m], place_of(2 * there + r, pair, c)
        )

    def send_low(there, r):
        g = (2 * order(there) + 7) % 8
        return remote(
            parcel.at[r, g], lows.at[m], below_sem.at[r, g], low_sem.at[m],
            place_of(2 * there + r, after if isinstance(there, int) else pair, 0),
        )

    def first_leg(act, own):
        for turn, dz in enumerate(AROUND):
            there = lax.rem(z + dz, 8)
            holds_high = order(there) // 4 == core
            holds_low = jnp.logical_and(lax.rem(order(there) + 7, 8) // 4 == core, order(there) != 0)
            for dx in (1, 0):
                r = lax.rem(x + dx, 2)
                same = dz == 0 and dx == 0

                @pl.when(holds_high)
                def _():
                    for c in range(2):
                        if same:
                            pl.when(core != c)(lambda c=c: act(send_high(there, r, c)))
                        else:
                            act(send_high(there, r, c))

                @pl.when(jnp.logical_and(holds_low, core == 1) if same else holds_low)
                def _():
                    act(send_low(there, r))

            if turn == OPEN:

                @pl.when(jnp.logical_and(core == 1, pair != pairs - 1))
                def _():
                    if own:
                        pl.semaphore_wait(open_sem, 1)
                    for r in range(2):
                        act(send_low(LOWEST, r))

        if own:

            @pl.when(holder == core)
            def _():
                pltpu.make_async_copy(parcel.at[x, chunk], highs.at[m], high_sem.at[m]).start()

            @pl.when(jnp.logical_and(core == 0, jnp.logical_and(w > 0, w < 5)))
            def _():
                pltpu.make_async_copy(parcel.at[x, lax.rem(2 * w + 7, 8)], lows.at[m], low_sem.at[m]).start()

    first_leg(lambda copy: copy.start(), True)

    def spread_rows(k, carry):
        at = pl.multiple_of((k // 8) * 128 + lax.rem(k + chunk, 8) * 16, 16)
        for an in range(4):
            for g in range(8):
                line = jnp.broadcast_to(t0[an, pl.ds(g * 32 + k, 1), :], (16, WIDE))
                line = pltpu.roll(line, 0, 1, stride=1, stride_axis=0)
                tt[an, g // 2, pl.ds(at, 16), (g % 2) * WIDE : (g % 2 + 1) * WIDE] = line.astype(BF16)
        return carry

    lax.fori_loop(0, 32, spread_rows, 0)

    high = row((PAIRS, ORB))
    small = lane((PAIRS, ORB))
    over = jnp.zeros((PAIRS, ORB), I32)
    for i in range(1, ORB):
        over += (high >= ORB * i).astype(I32)
    outer = (over == small).astype(F32).astype(BF16)
    inner = (high - ORB * over == small).astype(F32).astype(BF16)
    for an in range(4):
        block = c_ref[an // 2][:, an % 2, :]
        left = dot_t(dot(outer, block).astype(BF16), outer)
        right = dot_t(dot(inner, block).astype(BF16), inner)
        kron[an] = (left * right).astype(BF16)

    start = jnp.logical_and(jnp.logical_and(w == 0, core == 0), pair == 0)

    def passed_on(there):
        return remote(
            highs.at[there], lows.at[there], pass_sem.at[there], low_sem.at[there], place_of(m, pair, 1)
        )

    def arrived(buffer, sem, there):
        pltpu.make_async_copy(buffer.at[there], buffer.at[there], sem.at[there]).wait()

    even = ((place + chunk) & 1) == 1
    first_half = ((lane((PAIRS, WIDE)) - 16 * (chunk + 7)) & 127) < 64

    def merged(there):
        under = jnp.where(start, 0.0, lows[there].astype(F32))
        over = highs[there].astype(F32)
        upper = jnp.where(even, under, over)
        lower = pltpu.roll(jnp.where(even, over, under), WIDE - 16, 1)
        return jnp.concatenate([upper, lower], axis=0)

    def take(part):
        for i in range(4):
            arrived(highs, high_sem, 4 * part + i)

        @pl.when(core == 0)
        def _():
            for i in range(4):
                passed_on(4 * part + i).start()

    def convolve(part, fresh):
        for i in range(4):
            pl.when(jnp.logical_not(start))(lambda i=i: arrived(lows, low_sem, 4 * part + i))
        for g in range(2):
            near = merged(4 * part + 2 * g)
            far = merged(4 * part + 2 * g + 1)
            ga[0, :, g * WIDE : (g + 1) * WIDE] = jnp.where(first_half, near, far).astype(BF16)
            ga[1, :, g * WIDE : (g + 1) * WIDE] = jnp.where(first_half, far, near).astype(BF16)
        for an in range(4):
            term = dot_t(ga[nb_ref[an // 2, an % 2]], tt[an, part])
            acc[an] = term if fresh else acc[an] + term

    parts = [lax.rem(z // 2 + turn, 4) for turn in (2, 1, 3, 0)]
    lagging = jnp.logical_and(w == 0, core == 0)
    take(parts[0])

    @pl.when(lagging)
    def _():
        for i in range(1, 4):
            take(parts[i])

    for i in range(4):
        if i < 3:

            @pl.when(jnp.logical_not(lagging))
            def _():
                take(parts[i + 1])

        convolve(parts[i], i == 0)

    slot = 2 * chunk + x

    def back(there):
        return remote(
            send2.at[there], recv2.at[slot], send2_sem.at[there], recv2_sem.at[slot],
            place_of(there, pair, holder),
        )

    for g in (0, 1, 2, 3):
        done = []
        for a in range(2):
            total = None
            for an in (2 * a, 2 * a + 1):
                term = dot(kron[an], acc[an, :, g * WIDE : (g + 1) * WIDE].astype(BF16))
                total = term if total is None else total + term
            done.append(total)
        tiles = []
        for c in range(4):
            block = done[c % 2][HALF * (c // 2) : HALF * (c // 2 + 1)]
            tiles.append(pltpu.roll(block, 32 * c, 1) if c else block)
        for i in (0, 1, 2, 3):
            send2[4 * g + i] = pick(((place + 16 - chunk - 2 * i) & 7) >> 1, tiles).astype(BF16)
        for there in [4 * g + i for i in (0, 1, 2, 3)]:
            here = jnp.logical_and(m == there, holder == core)

            @pl.when(jnp.logical_not(here))
            def _():
                back(there).start()

            @pl.when(here)
            def _():
                pltpu.make_async_copy(send2.at[there], recv2.at[slot], recv2_sem.at[slot]).start()

    mine = lax.rem(m, 4)
    for r in range(2):
        for b in range(8):
            arrived(recv2, recv2_sem, 2 * b + r)
        blocks = [recv2[2 * b + r].astype(F32) for b in range(8)]
        halves = []
        for c in range(8):
            merged = pick((place + 16 - c - 2 * mine) & 7, blocks)
            halves.append(pltpu.roll(merged, (16 * (16 - c - 2 * mine)) & 127, 1))
        for a in range(2):
            for k in range(2):
                whole = jnp.concatenate([halves[2 * a + k], halves[4 + 2 * a + k]], axis=0)
                out_ref[k, a, r] = whole.astype(BF16)

    first_leg(lambda copy: copy.wait_send(), False)
    for there in range(16):

        @pl.when(jnp.logical_not(jnp.logical_and(m == there, holder == core)))
        def _():
            back(there).wait_send()


    @pl.when(core == 0)
    def _():
        for there in range(16):
            passed_on(there).wait_send()


def local(greens, phonon_kernel, coupling, neighbours, transfer_table, *, nen):
    vmem = pl.BlockSpec(memory_space=pltpu.VMEM)
    hbm = pl.BlockSpec(memory_space=pltpu.HBM)
    arguments = (
        greens.transpose(0, 1, 3, 4, 2, 5).reshape(2, 2, PAIRS, 2, WIDE),
        phonon_kernel.transpose(1, 2, 3, 0).reshape(64, 32),
        coupling.transpose(0, 2, 1, 3),
        neighbours,
        transfer_table,
    )
    out = pl.pallas_call(
        functools.partial(kernel, nen),
        out_shape=jax.ShapeDtypeStruct((2, 2, 2, PAIRS, WIDE), BF16),
        in_specs=[hbm] * 5,
        out_specs=vmem,
        scratch_shapes=[
            pltpu.VMEM((2, 2, PAIRS, 2, WIDE), BF16),
            pltpu.VMEM((64, 32), BF16),
            pltpu.VMEM((2, ORB, 2, ORB), BF16),
            pltpu.SMEM((2, 2), I32),
            pltpu.VMEM((32, 32), I32),
            pltpu.VMEM((2, 4, PAIRS, WIDE), F32),
            pltpu.VMEM((2, 8, HALF, WIDE), BF16),
            pltpu.VMEM((16, HALF, WIDE), BF16),
            pltpu.VMEM((16, HALF, WIDE), BF16),
            pltpu.VMEM((2, PAIRS, 2 * WIDE), BF16),
            pltpu.VMEM((4, 4, 512, 2 * WIDE), BF16),
            pltpu.VMEM((2, 256, WIDE), BF16),
            pltpu.VMEM((4, 256, WIDE), F32),
            pltpu.VMEM((4, PAIRS, PAIRS), BF16),
            pltpu.VMEM((4, PAIRS, 512), F32),
            pltpu.VMEM((16, HALF, WIDE), BF16),
            pltpu.VMEM((16, HALF, WIDE), BF16),
            pltpu.SemaphoreType.DMA((2, 8)),
            pltpu.SemaphoreType.DMA((2, 8)),
            pltpu.SemaphoreType.DMA((16,)),
            pltpu.SemaphoreType.DMA((16,)),
            pltpu.SemaphoreType.DMA((16,)),
            pltpu.SemaphoreType.DMA((16,)),
            pltpu.SemaphoreType.DMA((16,)),
            pltpu.SemaphoreType.DMA((5,)),
            pltpu.SemaphoreType.REGULAR,
        ],
        compiler_params=pltpu.CompilerParams(
            collective_id=0, has_side_effects=True, vmem_limit_bytes=32 * 2**20
        ),
    )(*(pltpu.with_memory_space_constraint(value, pltpu.HBM) for value in arguments))
    return out.reshape(greens.shape)


def solution(mesh):
    spec = P("mom", None, None, None, None, "en")
    return jax.shard_map(
        functools.partial(local, nen=mesh.shape["en"]),
        mesh=mesh,
        in_specs=(spec, P(), P(), P(), P()),
        out_specs=spec,
        check_vma=False,
    )
```

```python
import functools

import jax
import jax.numpy as jnp
from jax import lax
from jax.experimental import pallas as pl
from jax.experimental.pallas import tpu as pltpu
from jax.sharding import PartitionSpec as P

MESH = pl.DeviceIdType.MESH
F32 = jnp.float32
BF16 = jnp.bfloat16
I32 = jnp.int32

ORB = 12
PAIRS = 144
HALF = 72
WIDE = 128
LOWEST = 6
OPEN = 1
AROUND = (4, 3, 5, 2, 6, 1, 7, 0)


def order(z):
    return 4 * (z % 2) + (z // 2 + 1) % 4


def lane(shape):
    return lax.broadcasted_iota(I32, shape, len(shape) - 1)


def row(shape):
    return lax.broadcasted_iota(I32, shape, len(shape) - 2)


def pick(index, choices):
    out = choices[-1]
    for value in range(len(choices) - 2, -1, -1):
        out = jnp.where(index == value, choices[value], out)
    return out


def dot(a, b):
    return jnp.dot(a, b, preferred_element_type=F32)


def dot_t(a, b):
    return lax.dot_general(a, b, (((1,), (1,)), ((), ())), preferred_element_type=F32)


def kernel(
    nen, g_hbm, ph_hbm, c_hbm, nb_hbm, t_hbm, out_ref,
    g_ref, ph_ref, c_ref, nb_ref, t_ref,
    yt, parcel, lows, highs, ga, tt, ohs, t0, kron, acc, send2, recv2,
    home_sem, below_sem, low_sem, high_sem, pass_sem, send2_sem, recv2_sem, load_sems, open_sem,
):
    m = lax.axis_index("mom")
    q = lax.axis_index("en")
    z = m // 2
    w = order(z)
    x = m % 2
    core = q % 2
    pair = q // 2
    pairs = nen // 2
    chunk = lax.rem(2 * w + core, 8)
    holder = w // 4

    def place_of(there, pair_there, core_there):
        return {"mom": there, "en": 2 * pair_there + core_there}

    barrier = pltpu.get_barrier_semaphore()

    def greet(there, pair_there, core_there):
        pl.semaphore_signal(
            barrier, inc=1, device_id=place_of(there, pair_there, core_there), device_id_type=MESH
        )

    after = lax.rem(pair + 1, pairs)
    before = lax.rem(pair + pairs - 1, pairs)
    for dz in AROUND[:-1]:
        for dx in range(2):
            for c in range(2):
                greet(lax.rem(z + dz, 8) * 2 + lax.rem(x + dx, 2), pair, c)
    for c in range(2):
        greet(2 * z + 1 - x, pair, c)
    greet(m, pair, 1 - core)

    beside = jnp.where(core == 0, before, after)
    linked = jnp.where(core == 0, pair != 0, pair != pairs - 1)

    @pl.when(linked)
    def _():
        greet(m, beside, 1 - core)


    loads = [
        pltpu.make_async_copy(there, here, load_sems.at[i])
        for i, (there, here) in enumerate(
            [(g_hbm, g_ref), (ph_hbm, ph_ref), (c_hbm, c_ref), (nb_hbm, nb_ref), (t_hbm, t_ref)]
        )
    ]
    for load in loads:
        load.start()
    loads[0].wait()

    for c in range(4):
        both = g_ref[c % 2, lax.rem(c // 2 + x, 2)].astype(F32)
        for r in range(2):
            block = both[:, r, :]
            yt[r, c] = pltpu.roll(block, 32 * c, 1) if c else block

    place = lane((HALF, WIDE)) >> 4
    for r in range(2):
        for g in range(8):
            at = ((place + (8 - g)) & 7) >> 1
            upper = pick(at, [yt[r, c, :HALF, :] for c in range(4)])
            lower = pick(at, [yt[r, c, HALF:, :] for c in range(4)])
            parcel[r, g] = jnp.where(((place + g) & 1) == 0, upper, pltpu.roll(lower, 16, 1)).astype(BF16)

    for load in loads[1:]:
        load.wait()
    table = t_ref[...].astype(F32).astype(BF16)
    kk = row((32, WIDE))
    for v in range(2):
        for g in range(8):
            slot = lane((32, WIDE)) >> 5
            if v:
                slot = slot ^ 2
            spread = (kk == slot + 4 * g).astype(F32).astype(BF16)
            wanted = (lane((32, WIDE)) & 31).astype(F32)
            ohs[v, g * 32 : (g + 1) * 32, :] = (dot(table, spread) == wanted).astype(F32).astype(BF16)

    shifted = (lane((WIDE, WIDE)) - 16 * (chunk + 7)) & 127
    slot_match = (row((WIDE, WIDE)) >> 5) == (shifted >> 5)
    lag_at = ((lane((64, WIDE)) - 16 * (chunk + 7)) & 31)
    same = (row((32, 32)) == lane((32, 32))).astype(F32).astype(BF16)
    kernels = dot_t(same, ph_ref[...]).astype(BF16)
    for an in range(4):
        select = jnp.where(row((64, WIDE)) == 16 * an + 16 - lag_at, 1.0, 0.0)
        select = jnp.where(lag_at == 0, 0.0, jnp.where(lag_at > 16, 0.0, select)).astype(BF16)
        lags = dot(kernels, select)
        lags = jnp.concatenate([lags] * 4, axis=0)
        lags = jnp.where(slot_match, lags, 0.0).astype(BF16)
        t0[an] = dot(ohs[nb_ref[an // 2, an % 2]], lags)

    pl.semaphore_wait(barrier, 31 + linked.astype(I32))


    @pl.when(jnp.logical_and(core == 0, pair != 0))
    def _():
        pl.semaphore_signal(open_sem, inc=1, device_id=place_of(m, before, 1), device_id_type=MESH)

    def remote(source, target, send_sem, recv_sem, there):
        return pltpu.make_async_remote_copy(
            source, target, send_sem, recv_sem, device_id=there, device_id_type=MESH
        )

    def send_high(there, r, c):
        g = lax.rem(2 * order(there) + c, 8)
        return remote(
            parcel.at[r, g], highs.at[m], home_sem.at[r, g], high_sem.at[m], place_of(2 * there + r, pair, c)
        )

    def send_low(there, r):
        g = (2 * order(there) + 7) % 8
        return remote(
            parcel.at[r, g], lows.at[m], below_sem.at[r, g], low_sem.at[m],
            place_of(2 * there + r, after if isinstance(there, int) else pair, 0),
        )

    def first_leg(act, own):
        for turn, dz in enumerate(AROUND):
            there = lax.rem(z + dz, 8)
            holds_high = order(there) // 4 == core
            holds_low = jnp.logical_and(lax.rem(order(there) + 7, 8) // 4 == core, order(there) != 0)
            for dx in (1, 0):
                r = lax.rem(x + dx, 2)
                same = dz == 0 and dx == 0

                @pl.when(holds_high)
                def _():
                    for c in range(2):
                        if same:
                            pl.when(core != c)(lambda c=c: act(send_high(there, r, c)))
                        else:
                            act(send_high(there, r, c))

                @pl.when(jnp.logical_and(holds_low, core == 1) if same else holds_low)
                def _():
                    act(send_low(there, r))

            if turn == OPEN:

                @pl.when(jnp.logical_and(core == 1, pair != pairs - 1))
                def _():
                    if own:
                        pl.semaphore_wait(open_sem, 1)
                    for r in range(2):
                        act(send_low(LOWEST, r))

        if own:

            @pl.when(holder == core)
            def _():
                pltpu.make_async_copy(parcel.at[x, chunk], highs.at[m], high_sem.at[m]).start()

            @pl.when(jnp.logical_and(core == 0, jnp.logical_and(w > 0, w < 5)))
            def _():
                pltpu.make_async_copy(parcel.at[x, lax.rem(2 * w + 7, 8)], lows.at[m], low_sem.at[m]).start()

    first_leg(lambda copy: copy.start(), True)

    def spread_rows(k, carry):
        at = pl.multiple_of((k // 8) * 128 + lax.rem(k + chunk, 8) * 16, 16)
        for an in range(4):
            for g in range(8):
                line = jnp.broadcast_to(t0[an, pl.ds(g * 32 + k, 1), :], (16, WIDE))
                line = pltpu.roll(line, 0, 1, stride=1, stride_axis=0)
                tt[an, g // 2, pl.ds(at, 16), (g % 2) * WIDE : (g % 2 + 1) * WIDE] = line.astype(BF16)
        return carry

    lax.fori_loop(0, 32, spread_rows, 0)

    high = row((PAIRS, ORB))
    small = lane((PAIRS, ORB))
    over = jnp.zeros((PAIRS, ORB), I32)
    for i in range(1, ORB):
        over += (high >= ORB * i).astype(I32)
    outer = (over == small).astype(F32).astype(BF16)
    inner = (high - ORB * over == small).astype(F32).astype(BF16)
    for an in range(4):
        block = c_ref[an // 2][:, an % 2, :]
        left = dot_t(dot(outer, block).astype(BF16), outer)
        right = dot_t(dot(inner, block).astype(BF16), inner)
        kron[an] = (left * right).astype(BF16)

    start = jnp.logical_and(jnp.logical_and(w == 0, core == 0), pair == 0)

    def passed_on(there):
        return remote(
            highs.at[there], lows.at[there], pass_sem.at[there], low_sem.at[there], place_of(m, pair, 1)
        )

    def arrived(buffer, sem, there):
        pltpu.make_async_copy(buffer.at[there], buffer.at[there], sem.at[there]).wait()

    even = ((place + chunk) & 1) == 1
    first_half = ((lane((PAIRS, WIDE)) - 16 * (chunk + 7)) & 127) < 64

    def merged(there):
        under = jnp.where(start, 0.0, lows[there].astype(F32))
        over = highs[there].astype(F32)
        upper = jnp.where(even, under, over)
        lower = pltpu.roll(jnp.where(even, over, under), WIDE - 16, 1)
        return jnp.concatenate([upper, lower], axis=0)

    def take(part):
        for i in range(4):
            arrived(highs, high_sem, 4 * part + i)

        @pl.when(core == 0)
        def _():
            for i in range(4):
                passed_on(4 * part + i).start()

    def convolve(part, fresh):
        for i in range(4):
            pl.when(jnp.logical_not(start))(lambda i=i: arrived(lows, low_sem, 4 * part + i))
        for g in range(2):
            near = merged(4 * part + 2 * g)
            far = merged(4 * part + 2 * g + 1)
            ga[0, :, g * WIDE : (g + 1) * WIDE] = jnp.where(first_half, near, far).astype(BF16)
            ga[1, :, g * WIDE : (g + 1) * WIDE] = jnp.where(first_half, far, near).astype(BF16)
        for an in range(4):
            term = dot_t(ga[nb_ref[an // 2, an % 2]], tt[an, part])
            acc[an] = term if fresh else acc[an] + term

    parts = [lax.rem(z // 2 + turn, 4) for turn in (2, 1, 3, 0)]
    lagging = jnp.logical_and(w == 0, core == 0)
    take(parts[0])

    @pl.when(lagging)
    def _():
        for i in range(1, 4):
            take(parts[i])

    for i in range(4):
        if i < 3:

            @pl.when(jnp.logical_not(lagging))
            def _():
                take(parts[i + 1])

        convolve(parts[i], i == 0)

    slot = 2 * chunk + x

    def back(there):
        return remote(
            send2.at[there], recv2.at[slot], send2_sem.at[there], recv2_sem.at[slot],
            place_of(there, pair, holder),
        )

    for g in (0, 1, 2, 3):
        done = []
        for a in range(2):
            total = None
            for an in (2 * a, 2 * a + 1):
                term = dot(kron[an], acc[an, :, g * WIDE : (g + 1) * WIDE].astype(BF16))
                total = term if total is None else total + term
            done.append(total)
        tiles = []
        for c in range(4):
            block = done[c % 2][HALF * (c // 2) : HALF * (c // 2 + 1)]
            tiles.append(pltpu.roll(block, 32 * c, 1) if c else block)
        for i in (0, 1, 2, 3):
            send2[4 * g + i] = pick(((place + 16 - chunk - 2 * i) & 7) >> 1, tiles).astype(BF16)
        for there in [4 * g + i for i in (0, 1, 2, 3)]:
            here = jnp.logical_and(m == there, holder == core)

            @pl.when(jnp.logical_not(here))
            def _():
                back(there).start()

            @pl.when(here)
            def _():
                pltpu.make_async_copy(send2.at[there], recv2.at[slot], recv2_sem.at[slot]).start()

    first_leg(lambda copy: copy.wait_send(), False)
    @pl.when(core == 0)
    def _():
        for there in range(16):
            passed_on(there).wait_send()

    mine = lax.rem(m, 4)
    for r in range(2):
        for b in range(8):
            arrived(recv2, recv2_sem, 2 * b + r)
        blocks = [recv2[2 * b + r].astype(F32) for b in range(8)]
        halves = []
        for c in range(8):
            merged = pick((place + 16 - c - 2 * mine) & 7, blocks)
            halves.append(pltpu.roll(merged, (16 * (16 - c - 2 * mine)) & 127, 1))
        for a in range(2):
            for k in range(2):
                whole = jnp.concatenate([halves[2 * a + k], halves[4 + 2 * a + k]], axis=0)
                out_ref[k, a, r] = whole.astype(BF16)

    for there in range(16):

        @pl.when(jnp.logical_not(jnp.logical_and(m == there, holder == core)))
        def _():
            back(there).wait_send()


def local(greens, phonon_kernel, coupling, neighbours, transfer_table, *, nen):
    vmem = pl.BlockSpec(memory_space=pltpu.VMEM)
    hbm = pl.BlockSpec(memory_space=pltpu.HBM)
    arguments = (
        greens.transpose(0, 1, 3, 4, 2, 5).reshape(2, 2, PAIRS, 2, WIDE),
        phonon_kernel.transpose(1, 2, 3, 0).reshape(64, 32),
        coupling.transpose(0, 2, 1, 3),
        neighbours,
        transfer_table,
    )
    out = pl.pallas_call(
        functools.partial(kernel, nen),
        out_shape=jax.ShapeDtypeStruct((2, 2, 2, PAIRS, WIDE), BF16),
        in_specs=[hbm] * 5,
        out_specs=vmem,
        scratch_shapes=[
            pltpu.VMEM((2, 2, PAIRS, 2, WIDE), BF16),
            pltpu.VMEM((64, 32), BF16),
            pltpu.VMEM((2, ORB, 2, ORB), BF16),
            pltpu.SMEM((2, 2), I32),
            pltpu.VMEM((32, 32), I32),
            pltpu.VMEM((2, 4, PAIRS, WIDE), F32),
            pltpu.VMEM((2, 8, HALF, WIDE), BF16),
            pltpu.VMEM((16, HALF, WIDE), BF16),
            pltpu.VMEM((16, HALF, WIDE), BF16),
            pltpu.VMEM((2, PAIRS, 2 * WIDE), BF16),
            pltpu.VMEM((4, 4, 512, 2 * WIDE), BF16),
            pltpu.VMEM((2, 256, WIDE), BF16),
            pltpu.VMEM((4, 256, WIDE), F32),
            pltpu.VMEM((4, PAIRS, PAIRS), BF16),
            pltpu.VMEM((4, PAIRS, 512), F32),
            pltpu.VMEM((16, HALF, WIDE), BF16),
            pltpu.VMEM((16, HALF, WIDE), BF16),
            pltpu.SemaphoreType.DMA((2, 8)),
            pltpu.SemaphoreType.DMA((2, 8)),
            pltpu.SemaphoreType.DMA((16,)),
            pltpu.SemaphoreType.DMA((16,)),
            pltpu.SemaphoreType.DMA((16,)),
            pltpu.SemaphoreType.DMA((16,)),
            pltpu.SemaphoreType.DMA((16,)),
            pltpu.SemaphoreType.DMA((5,)),
            pltpu.SemaphoreType.REGULAR,
        ],
        compiler_params=pltpu.CompilerParams(
            collective_id=0, has_side_effects=True, vmem_limit_bytes=32 * 2**20
        ),
    )(*(pltpu.with_memory_space_constraint(value, pltpu.HBM) for value in arguments))
    return out.reshape(greens.shape)


def solution(mesh):
    spec = P("mom", None, None, None, None, "en")
    return jax.shard_map(
        functools.partial(local, nen=mesh.shape["en"]),
        mesh=mesh,
        in_specs=(spec, P(), P(), P(), P()),
        out_specs=spec,
        check_vma=False,
    )
```

```python
import functools

import jax
import jax.numpy as jnp
from jax import lax
from jax.experimental import pallas as pl
from jax.experimental.pallas import tpu as pltpu
from jax.sharding import PartitionSpec as P

MESH = pl.DeviceIdType.MESH
F32 = jnp.float32
BF16 = jnp.bfloat16
I32 = jnp.int32

ORB = 12
PAIRS = 144
HALF = 72
WIDE = 128
LOWEST = 6
OPEN = 1
AROUND = (4, 3, 5, 2, 6, 1, 7, 0)


def order(z):
    return 4 * (z % 2) + (z // 2 + 1) % 4


def lane(shape):
    return lax.broadcasted_iota(I32, shape, len(shape) - 1)


def row(shape):
    return lax.broadcasted_iota(I32, shape, len(shape) - 2)


def pick(index, choices):
    out = choices[-1]
    for value in range(len(choices) - 2, -1, -1):
        out = jnp.where(index == value, choices[value], out)
    return out


def dot(a, b):
    return jnp.dot(a, b, preferred_element_type=F32)


def dot_t(a, b):
    return lax.dot_general(a, b, (((1,), (1,)), ((), ())), preferred_element_type=F32)


def kernel(
    nen, g_hbm, ph_hbm, c_hbm, nb_hbm, t_hbm, out_ref,
    g_ref, ph_ref, c_ref, nb_ref, t_ref,
    yt, parcel, lows, highs, ga, tt, ohs, t0, kron, acc, send2, recv2,
    home_sem, below_sem, low_sem, high_sem, pass_sem, send2_sem, recv2_sem, load_sems, open_sem,
):
    m = lax.axis_index("mom")
    q = lax.axis_index("en")
    z = m // 2
    w = order(z)
    x = m % 2
    core = q % 2
    pair = q // 2
    pairs = nen // 2
    chunk = lax.rem(2 * w + core, 8)
    holder = w // 4

    def place_of(there, pair_there, core_there):
        return {"mom": there, "en": 2 * pair_there + core_there}

    barrier = pltpu.get_barrier_semaphore()

    def greet(there, pair_there, core_there):
        pl.semaphore_signal(
            barrier, inc=1, device_id=place_of(there, pair_there, core_there), device_id_type=MESH
        )

    after = lax.rem(pair + 1, pairs)
    before = lax.rem(pair + pairs - 1, pairs)
    for dz in AROUND[:-1]:
        for dx in range(2):
            for c in range(2):
                greet(lax.rem(z + dz, 8) * 2 + lax.rem(x + dx, 2), pair, c)
    for c in range(2):
        greet(2 * z + 1 - x, pair, c)
    greet(m, pair, 1 - core)

    beside = jnp.where(core == 0, before, after)
    linked = jnp.where(core == 0, pair != 0, pair != pairs - 1)

    @pl.when(linked)
    def _():
        greet(m, beside, 1 - core)


    loads = [
        pltpu.make_async_copy(there, here, load_sems.at[i])
        for i, (there, here) in enumerate(
            [(g_hbm, g_ref), (ph_hbm, ph_ref), (c_hbm, c_ref), (nb_hbm, nb_ref), (t_hbm, t_ref)]
        )
    ]
    for load in loads:
        load.start()
    loads[0].wait()

    for c in range(4):
        both = g_ref[c % 2, lax.rem(c // 2 + x, 2)].astype(F32)
        for r in range(2):
            block = both[:, r, :]
            yt[r, c] = pltpu.roll(block, 32 * c, 1) if c else block

    place = lane((HALF, WIDE)) >> 4
    for r in range(2):
        for g in range(8):
            at = ((place + (8 - g)) & 7) >> 1
            upper = pick(at, [yt[r, c, :HALF, :] for c in range(4)])
            lower = pick(at, [yt[r, c, HALF:, :] for c in range(4)])
            parcel[r, g] = jnp.where(((place + g) & 1) == 0, upper, pltpu.roll(lower, 16, 1)).astype(BF16)

    for load in loads[1:]:
        load.wait()
    table = t_ref[...].astype(F32).astype(BF16)
    kk = row((32, WIDE))
    for v in range(2):
        for g in range(8):
            slot = lane((32, WIDE)) >> 5
            if v:
                slot = slot ^ 2
            spread = (kk == slot + 4 * g).astype(F32).astype(BF16)
            wanted = (lane((32, WIDE)) & 31).astype(F32)
            ohs[v, g * 32 : (g + 1) * 32, :] = (dot(table, spread) == wanted).astype(F32).astype(BF16)

    shifted = (lane((WIDE, WIDE)) - 16 * (chunk + 7)) & 127
    slot_match = (row((WIDE, WIDE)) >> 5) == (shifted >> 5)
    lag_at = ((lane((64, WIDE)) - 16 * (chunk + 7)) & 31)
    same = (row((32, 32)) == lane((32, 32))).astype(F32).astype(BF16)
    kernels = dot_t(same, ph_ref[...]).astype(BF16)
    for an in range(4):
        select = jnp.where(row((64, WIDE)) == 16 * an + 16 - lag_at, 1.0, 0.0)
        select = jnp.where(lag_at == 0, 0.0, jnp.where(lag_at > 16, 0.0, select)).astype(BF16)
        lags = dot(kernels, select)
        lags = jnp.concatenate([lags] * 4, axis=0)
        lags = jnp.where(slot_match, lags, 0.0).astype(BF16)
        t0[an] = dot(ohs[nb_ref[an // 2, an % 2]], lags)

    pl.semaphore_wait(barrier, 31 + linked.astype(I32))


    @pl.when(jnp.logical_and(core == 0, pair != 0))
    def _():
        pl.semaphore_signal(open_sem, inc=1, device_id=place_of(m, before, 1), device_id_type=MESH)

    def remote(source, target, send_sem, recv_sem, there):
        return pltpu.make_async_remote_copy(
            source, target, send_sem, recv_sem, device_id=there, device_id_type=MESH
        )

    def send_high(there, r, c):
        g = lax.rem(2 * order(there) + c, 8)
        return remote(
            parcel.at[r, g], highs.at[m], home_sem.at[r, g], high_sem.at[m], place_of(2 * there + r, pair, c)
        )

    def send_low(there, r):
        g = (2 * order(there) + 7) % 8
        return remote(
            parcel.at[r, g], lows.at[m], below_sem.at[r, g], low_sem.at[m],
            place_of(2 * there + r, after if isinstance(there, int) else pair, 0),
        )

    def first_leg(act, own):
        for turn, dz in enumerate(AROUND):
            there = lax.rem(z + dz, 8)
            holds_high = order(there) // 4 == core
            holds_low = jnp.logical_and(lax.rem(order(there) + 7, 8) // 4 == core, order(there) != 0)
            for dx in (1, 0):
                r = lax.rem(x + dx, 2)
                same = dz == 0 and dx == 0

                @pl.when(holds_high)
                def _():
                    for c in range(2):
                        if same:
                            pl.when(core != c)(lambda c=c: act(send_high(there, r, c)))
                        else:
                            act(send_high(there, r, c))

                @pl.when(jnp.logical_and(holds_low, core == 1) if same else holds_low)
                def _():
                    act(send_low(there, r))

            if turn == OPEN:

                @pl.when(jnp.logical_and(core == 1, pair != pairs - 1))
                def _():
                    if own:
                        pl.semaphore_wait(open_sem, 1)
                    for r in range(2):
                        act(send_low(LOWEST, r))

        if own:

            @pl.when(holder == core)
            def _():
                pltpu.make_async_copy(parcel.at[x, chunk], highs.at[m], high_sem.at[m]).start()

            @pl.when(jnp.logical_and(core == 0, jnp.logical_and(w > 0, w < 5)))
            def _():
                pltpu.make_async_copy(parcel.at[x, lax.rem(2 * w + 7, 8)], lows.at[m], low_sem.at[m]).start()

    first_leg(lambda copy: copy.start(), True)

    def spread_rows(k, carry):
        at = pl.multiple_of((k // 8) * 128 + lax.rem(k + chunk, 8) * 16, 16)
        for an in range(4):
            for g in range(8):
                line = jnp.broadcast_to(t0[an, pl.ds(g * 32 + k, 1), :], (16, WIDE))
                line = pltpu.roll(line, 0, 1, stride=1, stride_axis=0)
                tt[an, g // 2, pl.ds(at, 16), (g % 2) * WIDE : (g % 2 + 1) * WIDE] = line.astype(BF16)
        return carry

    lax.fori_loop(0, 32, spread_rows, 0)

    high = row((PAIRS, ORB))
    small = lane((PAIRS, ORB))
    over = jnp.zeros((PAIRS, ORB), I32)
    for i in range(1, ORB):
        over += (high >= ORB * i).astype(I32)
    outer = (over == small).astype(F32).astype(BF16)
    inner = (high - ORB * over == small).astype(F32).astype(BF16)
    for an in range(4):
        block = c_ref[an // 2][:, an % 2, :]
        left = dot_t(dot(outer, block).astype(BF16), outer)
        right = dot_t(dot(inner, block).astype(BF16), inner)
        kron[an] = (left * right).astype(BF16)

    start = jnp.logical_and(jnp.logical_and(w == 0, core == 0), pair == 0)

    def passed_on(there):
        return remote(
            highs.at[there], lows.at[there], pass_sem.at[there], low_sem.at[there], place_of(m, pair, 1)
        )

    def arrived(buffer, sem, there):
        pltpu.make_async_copy(buffer.at[there], buffer.at[there], sem.at[there]).wait()

    even = ((place + chunk) & 1) == 1
    first_half = ((lane((PAIRS, WIDE)) - 16 * (chunk + 7)) & 127) < 64

    def merged(there):
        under = jnp.where(start, 0.0, lows[there].astype(F32))
        over = highs[there].astype(F32)
        upper = jnp.where(even, under, over)
        lower = pltpu.roll(jnp.where(even, over, under), WIDE - 16, 1)
        return jnp.concatenate([upper, lower], axis=0)

    def take(part):
        for i in range(4):
            arrived(highs, high_sem, 4 * part + i)

        @pl.when(core == 0)
        def _():
            for i in range(4):
                passed_on(4 * part + i).start()

    def convolve(part, fresh):
        for i in range(4):
            pl.when(jnp.logical_not(start))(lambda i=i: arrived(lows, low_sem, 4 * part + i))
        for g in range(2):
            near = merged(4 * part + 2 * g)
            far = merged(4 * part + 2 * g + 1)
            ga[0, :, g * WIDE : (g + 1) * WIDE] = jnp.where(first_half, near, far).astype(BF16)
            ga[1, :, g * WIDE : (g + 1) * WIDE] = jnp.where(first_half, far, near).astype(BF16)
        for an in range(4):
            term = dot_t(ga[nb_ref[an // 2, an % 2]], tt[an, part])
            acc[an] = term if fresh else acc[an] + term

    parts = [lax.rem(z // 2 + turn, 4) for turn in (0, 2, 3, 1)]
    lagging = jnp.logical_and(w == 0, core == 0)
    take(parts[0])

    @pl.when(lagging)
    def _():
        for i in range(1, 4):
            take(parts[i])

    for i in range(4):
        if i < 3:

            @pl.when(jnp.logical_not(lagging))
            def _():
                take(parts[i + 1])

        convolve(parts[i], i == 0)

    slot = 2 * chunk + x

    def back(there):
        return remote(
            send2.at[there], recv2.at[slot], send2_sem.at[there], recv2_sem.at[slot],
            place_of(there, pair, holder),
        )

    for g in (0, 1, 2, 3):
        done = []
        for a in range(2):
            total = None
            for an in (2 * a, 2 * a + 1):
                term = dot(kron[an], acc[an, :, g * WIDE : (g + 1) * WIDE].astype(BF16))
                total = term if total is None else total + term
            done.append(total)
        tiles = []
        for c in range(4):
            block = done[c % 2][HALF * (c // 2) : HALF * (c // 2 + 1)]
            tiles.append(pltpu.roll(block, 32 * c, 1) if c else block)
        for i in (0, 1, 2, 3):
            send2[4 * g + i] = pick(((place + 16 - chunk - 2 * i) & 7) >> 1, tiles).astype(BF16)
        for there in [4 * g + i for i in (0, 1, 2, 3)]:
            here = jnp.logical_and(m == there, holder == core)

            @pl.when(jnp.logical_not(here))
            def _():
                back(there).start()

            @pl.when(here)
            def _():
                pltpu.make_async_copy(send2.at[there], recv2.at[slot], recv2_sem.at[slot]).start()

    first_leg(lambda copy: copy.wait_send(), False)
    @pl.when(core == 0)
    def _():
        for there in range(16):
            passed_on(there).wait_send()

    mine = lax.rem(m, 4)
    for r in range(2):
        for b in range(8):
            arrived(recv2, recv2_sem, 2 * b + r)
        blocks = [recv2[2 * b + r].astype(F32) for b in range(8)]
        halves = []
        for c in range(8):
            merged = pick((place + 16 - c - 2 * mine) & 7, blocks)
            halves.append(pltpu.roll(merged, (16 * (16 - c - 2 * mine)) & 127, 1))
        for a in range(2):
            for k in range(2):
                whole = jnp.concatenate([halves[2 * a + k], halves[4 + 2 * a + k]], axis=0)
                out_ref[k, a, r] = whole.astype(BF16)

    for there in range(16):

        @pl.when(jnp.logical_not(jnp.logical_and(m == there, holder == core)))
        def _():
            back(there).wait_send()


def local(greens, phonon_kernel, coupling, neighbours, transfer_table, *, nen):
    vmem = pl.BlockSpec(memory_space=pltpu.VMEM)
    hbm = pl.BlockSpec(memory_space=pltpu.HBM)
    arguments = (
        greens.transpose(0, 1, 3, 4, 2, 5).reshape(2, 2, PAIRS, 2, WIDE),
        phonon_kernel.transpose(1, 2, 3, 0).reshape(64, 32),
        coupling.transpose(0, 2, 1, 3),
        neighbours,
        transfer_table,
    )
    out = pl.pallas_call(
        functools.partial(kernel, nen),
        out_shape=jax.ShapeDtypeStruct((2, 2, 2, PAIRS, WIDE), BF16),
        in_specs=[hbm] * 5,
        out_specs=vmem,
        scratch_shapes=[
            pltpu.VMEM((2, 2, PAIRS, 2, WIDE), BF16),
            pltpu.VMEM((64, 32), BF16),
            pltpu.VMEM((2, ORB, 2, ORB), BF16),
            pltpu.SMEM((2, 2), I32),
            pltpu.VMEM((32, 32), I32),
            pltpu.VMEM((2, 4, PAIRS, WIDE), F32),
            pltpu.VMEM((2, 8, HALF, WIDE), BF16),
            pltpu.VMEM((16, HALF, WIDE), BF16),
            pltpu.VMEM((16, HALF, WIDE), BF16),
            pltpu.VMEM((2, PAIRS, 2 * WIDE), BF16),
            pltpu.VMEM((4, 4, 512, 2 * WIDE), BF16),
            pltpu.VMEM((2, 256, WIDE), BF16),
            pltpu.VMEM((4, 256, WIDE), F32),
            pltpu.VMEM((4, PAIRS, PAIRS), BF16),
            pltpu.VMEM((4, PAIRS, 512), F32),
            pltpu.VMEM((16, HALF, WIDE), BF16),
            pltpu.VMEM((16, HALF, WIDE), BF16),
            pltpu.SemaphoreType.DMA((2, 8)),
            pltpu.SemaphoreType.DMA((2, 8)),
            pltpu.SemaphoreType.DMA((16,)),
            pltpu.SemaphoreType.DMA((16,)),
            pltpu.SemaphoreType.DMA((16,)),
            pltpu.SemaphoreType.DMA((16,)),
            pltpu.SemaphoreType.DMA((16,)),
            pltpu.SemaphoreType.DMA((5,)),
            pltpu.SemaphoreType.REGULAR,
        ],
        compiler_params=pltpu.CompilerParams(
            collective_id=0, has_side_effects=True, vmem_limit_bytes=32 * 2**20
        ),
    )(*(pltpu.with_memory_space_constraint(value, pltpu.HBM) for value in arguments))
    return out.reshape(greens.shape)


def solution(mesh):
    spec = P("mom", None, None, None, None, "en")
    return jax.shard_map(
        functools.partial(local, nen=mesh.shape["en"]),
        mesh=mesh,
        in_specs=(spec, P(), P(), P(), P()),
        out_specs=spec,
        check_vma=False,
    )
```
